256 devices in a mesh: ctx: 16 (over x, y), head: 16 (over z, core).
Axes of the slice: x: 4, y: 4, z: 8, core: 2. Of those that a mesh axis runs over, the one named last changes fastest.
Arguments:
- tokens: bfloat16 [8192, 8192], P('ctx'), may hold values from -6 to 6
- w_zx: bfloat16 [8192, 2, 8192], P('ctx', None, 'head'), may hold values from -0.0625 to 0.0625
- zx_scale: float32 [2, 8192], P(None, 'head'), may hold values from 0.5 to 2
- w_bc: bfloat16 [8192, 8, 512], P('ctx'), may hold values from -0.0625 to 0.0625
- bc_scale: float32 [8, 512], replicated, may hold values from 0.5 to 2
- w_dt: bfloat16 [8192, 128], P('ctx', 'head'), may hold values from -0.0625 to 0.0625
- conv_x: float32 [5, 8192], P(None, 'head'), may hold values from -3 to 3
- conv_bc: float32 [5, 8, 512], replicated, may hold values from -3 to 3
- tail_x: bfloat16 [3, 8192], P(None, 'head'), may hold values from -6 to 6
- tail_bc: bfloat16 [3, 8, 512], replicated, may hold values from -6 to 6
- head_params: float32 [3, 128], P(None, 'head'), may hold values from -12 to 2, as said below
- init_state: float32 [128, 64, 256], P('head'), may hold values from -1.5 to 1.5
- norm_gain: float32 [8192], P('head'), may hold values from 0.5 to 1.5
Outputs:
- mixed: bfloat16 [8192, 8192], P('ctx', 'head')
The draws below stay inside these ranges and needn't reach their ends.
Inputs may be any that keep to these rules, and one draw needn't show every extreme that they name: `head_params`: row 0 lies in -3.5 to -2.5 and row 2 in 0.5 to 1.5.
All inputs are finite; a program needn't handle non-finite values.
Results may differ from the reference program's by a relative error of at most 0.0052.
Values may be sent and summed in bfloat16 or wider, within the bound.
A program may use at most 256 MiB of HBM per device.

```python
import math
import jax
import jax.numpy as jnp
from jax import lax

D = 8192
H = 128
P_SIZE = 64
N = 256
G = 8
K = 4
TOK_DEV = 512
TOKENS = 8192
DI = 8192


def draw_head_params(key, part):
    keys = jax.random.split(key, 5)
    quick_share = 0.5
    quick = jax.random.bernoulli(keys[0], quick_share, (H,))
    bias_row = jax.random.uniform(keys[1], (H,), jnp.float32, -3.5, -2.5)
    quick_rate = jnp.exp(jax.random.uniform(keys[2], (H,), jnp.float32, jnp.log(0.4), jnp.log(1.2)))
    slow_rate = jnp.exp(jax.random.uniform(keys[3], (H,), jnp.float32, jnp.log(0.2), jnp.log(1.0))) / (0.07 * TOKENS)
    rate_row = jnp.log(jnp.where(quick, quick_rate, slow_rate))
    skip_row = jax.random.uniform(keys[4], (H,), jnp.float32, 0.5, 1.5)
    return jnp.stack([bias_row, rate_row, skip_row]).astype(jnp.float32)


def steps_of(own_key, extent, cuts, smallest, largest):
    level, own = 1.0, jax.random.fold_in(own_key, 6)
    for dim, parts in cuts:
        draws = jnp.exp(jax.random.uniform(jax.random.fold_in(own, dim), (parts,), jnp.float32, smallest / len(cuts), largest / len(cuts)))
        level = level * jnp.repeat(draws, extent[dim] // parts).reshape([-1 if axis == dim else 1 for axis in range(len(extent))])
    return level


def centred(rng, dims, scale, reach, cuts=(), dtype=jnp.bfloat16):
    drawn = scale * jax.random.normal(rng, dims, jnp.float32)
    if cuts:
        drawn = drawn * steps_of(rng, dims, cuts, -0.22, 0.18)
    return jnp.clip(drawn, -reach, reach).astype(dtype)


def setup_inputs(seed: int = 0) -> dict:
    splits = jax.random.split(jax.random.key(seed), 14)
    tokens = centred(splits[0], (TOKENS, D), 1.0, 6.0, ((0, 16),))
    w_zx = centred(splits[1], (D, 2, DI), D ** -0.5, 0.0625, ((0, 16), (2, 16)))
    zx_scale = jnp.clip(jnp.exp(math.log(2.0) - 1.3862944 * jax.random.uniform(splits[2], (2, DI), jnp.float32) ** steps_of(splits[2], (2, DI), ((1, 16),), -0.2, 0.2)), 0.5, 2.0)
    w_bc = centred(splits[3], (D, G, 2 * N), D ** -0.5, 0.0625, ((0, 16),))
    bc_scale = jnp.clip(jnp.exp(jax.random.uniform(splits[4], (G, 2 * N), jnp.float32, math.log(0.5), math.log(2.0))), 0.5, 2.0)
    w_dt = centred(splits[5], (D, H), D ** -0.5, 0.0625, ((0, 16), (1, 16)))
    conv_x = centred(splits[6], (K + 1, DI), 0.5, 3.0, ((1, 16),), jnp.float32)
    conv_bc = centred(splits[7], (K + 1, G, 2 * N), 0.5, 3.0, (), jnp.float32)
    tail_x = centred(splits[8], (K - 1, DI), 1.0, 6.0, ((1, 16),))
    tail_bc = centred(splits[9], (K - 1, G, 2 * N), 1.0, 6.0)
    head_params = draw_head_params(jax.random.fold_in(splits[13], 71), 0)
    init_state = centred(splits[11], (H, P_SIZE, N), 0.1, 1.5, ((0, 16),), jnp.float32)
    norm_gain = jnp.clip(1.0 + 0.1 * jax.random.normal(splits[12], (DI,), jnp.float32), 0.5, 1.5)
    return dict(tokens=tokens, w_zx=w_zx, zx_scale=zx_scale, w_bc=w_bc, bc_scale=bc_scale, w_dt=w_dt, conv_x=conv_x, conv_bc=conv_bc, tail_x=tail_x, tail_bc=tail_bc, head_params=head_params, init_state=init_state, norm_gain=norm_gain)


def conv_silu(values, before, taps):
    length = values.shape[0]
    padded = jnp.concatenate([before, values], 0).astype(jnp.float32)
    summed = taps[K]
    for tap_index in range(K):
        summed = summed + taps[tap_index] * padded[tap_index:tap_index + length]
    return jax.nn.silu(summed).astype(jnp.bfloat16)

def block_step(state, inputs):
    x_blk, b_blk, c_blk, rate_blk, step_blk = inputs
    highest = lax.Precision.HIGHEST
    cumul = jnp.cumsum(rate_blk, 0)
    length = x_blk.shape[0]
    order = jnp.arange(length)
    lower = (order[:, None] >= order[None, :])[:, :, None, None]
    spread = cumul[:, None] - cumul[None, :]
    decay = jnp.where(lower, jnp.exp(jnp.minimum(spread, 0.0)), 0.0)
    scores = jnp.einsum('tgn,sgn->tsg', c_blk, b_blk, precision=highest)
    weights = decay * scores[:, :, :, None] * step_blk[None]
    inner = jnp.einsum('tsgh,sghp->tghp', weights, x_blk, precision=highest)
    carried = jnp.einsum('tgn,ghpn->tghp', c_blk, state, precision=highest) * jnp.exp(cumul)[..., None]
    final = cumul[length - 1]
    fade = jnp.exp(final[None] - cumul) * step_blk
    new_state = jnp.exp(final)[..., None, None] * state + jnp.einsum('sgh,sghp,sgn->ghpn', fade, x_blk, b_blk, precision=highest)
    return (new_state, inner + carried)

def reference(tokens, w_zx, zx_scale, w_bc, bc_scale, w_dt, conv_x, conv_bc, tail_x, tail_bc, head_params, init_state, norm_gain):
    per_group = H // G
    zx_val = jnp.dot(tokens, w_zx.reshape(D, 2 * DI), preferred_element_type=jnp.float32).reshape(TOKENS, 2, DI)
    zx_val = (zx_val * zx_scale).astype(jnp.bfloat16)
    bc_val = jnp.dot(tokens, w_bc.reshape(D, G * 2 * N), preferred_element_type=jnp.float32).reshape(TOKENS, G, 2 * N)
    bc_val = (bc_val * bc_scale).astype(jnp.bfloat16)
    step_size = jax.nn.softplus(jnp.dot(tokens, w_dt, preferred_element_type=jnp.float32) + head_params[0])
    xconv = conv_silu(zx_val[:, 1], tail_x, conv_x)
    bconv = conv_silu(bc_val, tail_bc, conv_bc)
    rate = -jnp.exp(head_params[1]) * step_size
    block_len = math.gcd(TOK_DEV, 256)
    blocks = TOKENS // block_len
    x_all = xconv.astype(jnp.float32).reshape(blocks, block_len, G, per_group, P_SIZE)
    b_all = bconv[:, :, :N].astype(jnp.float32).reshape(blocks, block_len, G, N)
    c_all = bconv[:, :, N:].astype(jnp.float32).reshape(blocks, block_len, G, N)
    rate_all = rate.reshape(blocks, block_len, G, per_group)
    step_all = step_size.reshape(blocks, block_len, G, per_group)
    start = init_state.reshape(G, per_group, P_SIZE, N)
    final_state, outputs = lax.scan(block_step, start, (x_all, b_all, c_all, rate_all, step_all))
    skipped = head_params[2].reshape(G, per_group)[None, None, :, :, None] * x_all
    y_val = (outputs + skipped).reshape(TOKENS, G, per_group * P_SIZE)
    gate = zx_val[:, 0].astype(jnp.float32).reshape(TOKENS, G, per_group * P_SIZE)
    gated = y_val * jax.nn.silu(gate)
    meansq = lax.optimization_barrier(jnp.mean(gated * gated, axis=-1, keepdims=True))
    mixed = gated * lax.rsqrt(meansq + 1e-05) * norm_gain.reshape(G, per_group * P_SIZE)
    return mixed.reshape(TOKENS, DI).astype(jnp.bfloat16)
```

```python
import jax
import jax.numpy as jnp
from jax import lax
from jax.experimental import pallas as pl
from jax.experimental.pallas import tpu as pltpu
from jax.sharding import PartitionSpec as P

H = 128
P_SIZE = 64
N = 256
G = 8
K = 4
MESH = pl.DeviceIdType.MESH
HALO = 16
NT = (((1,), (1,)), ((), ()))
TN = (((0,), (0,)), ((), ()))
JS = (0, 1, -1, 2)
ROWS = (((0, 128, 256), (256, 384, 528)), ((0, 128, 256), (256, 384, 512)))


def kernel(tok_hbm, w1_hbm, w2_hbm, *refs):
    small_in, out, small, refs = refs[:9], refs[9], refs[10:19], refs[19:]
    zxs, bcs, convx, convbc, tailx, tailbc, hp, gain, init = small
    (
        par, tok, w1, w2, acc1, acc2, accd, wp, ext, xb, bcb, gs, yb, cum, cumt, dtt,
        st1, rc1, st2, rc2, sq,
        wsend, wrecv, as1, ar1, as2, ar2, psend, precv, hsend, hrecv, lsem, ssem,
    ) = refs
    f32, bf16 = jnp.float32, jnp.bfloat16
    me = lax.axis_index("ctx")
    hd = lax.axis_index("head")
    core = lax.rem(hd, 2)
    mate = hd + 1 - 2 * core
    mx, my = me // 4, lax.rem(me, 4)

    def at(half, da, db):
        ox = half * da + (1 - half) * db
        oy = (1 - half) * da + half * db
        return lax.rem(mx + ox + 4, 4) * 4 + lax.rem(my + oy + 4, 4)

    barrier = pltpu.get_barrier_semaphore()
    for o in range(1, 16):
        pl.semaphore_signal(
            barrier, inc=1, device_id={"ctx": lax.rem(me + o, 16)}, device_id_type=MESH
        )
    pl.semaphore_signal(barrier, inc=1, device_id={"head": mate}, device_id_type=MESH)

    tok_in = pltpu.make_async_copy(tok_hbm, tok.at[pl.ds(0, 512), :], lsem.at[0])
    w1_in = pltpu.make_async_copy(w1_hbm, w1.at[me], lsem.at[1])
    w2_in = pltpu.make_async_copy(w2_hbm, w2.at[me], lsem.at[2])
    w1_in.start()
    tok_in.start()
    w2_in.start()
    small_copies = [
        pltpu.make_async_copy(a, b, ssem.at[n]) for n, (a, b) in enumerate(zip(small_in, small))
    ]
    for c in small_copies:
        c.start()
    pl.semaphore_wait(barrier, 16)

    sent = []

    def remote(src, dst, ssem, rsem, who):
        c = pltpu.make_async_remote_copy(
            src_ref=src, dst_ref=dst, send_sem=ssem, recv_sem=rsem,
            device_id=who, device_id_type=MESH,
        )
        sent.append(c)
        return c

    made = {}

    def weight(kind, half, phase, j, d):
        key = (kind, half, phase, j, d)
        if key in made:
            return made[key]
        index = len(made)
        start, split, end = ROWS[kind][half]
        if phase in (1, 3):
            start, end = (start, split) if d == 1 else (split, end)
        da, db = ((0, 0), (-d, 0), (j, 0), (j, -d))[phase]
        origin = at(half, da, db)
        who = at(half, d, 0) if phase < 2 else at(half, 0, d)
        rows = pl.ds(start, end - start)
        buf = (w1, w2)[kind]
        src = buf.at[origin, rows, :]
        if (da, db) == (0, 0):
            src = (w1_hbm, w2_hbm)[kind].at[rows, :]
        made[key] = remote(
            src, buf.at[origin, rows, :], wsend.at[index], wrecv.at[index], {"ctx": who}
        )
        return made[key]

    hd2 = [(half, d) for half in (0, 1) for d in (1, -1)]

    def issue(kind, step):
        todo = {
            0: [(0, (0,)), (2, (0,))],
            1: [(1, (0,)), (2, (1, -1))],
            2: [(3, (0,))],
            3: [(2, (2,))],
            4: [(3, (1, -1))],
            5: [(3, (2,))],
        }[step]
        for phase, js in todo:
            for j in js:
                for half, d in hd2:
                    weight(kind, half, phase, j, d).start()

    def arrive(kind, step):
        todo = {
            1: [(0, (0,))],
            2: [(2, (0,))],
            3: [(1, (0,))],
            4: [(2, (1, -1))],
            5: [(2, (2,))],
            6: [(3, (0, 1, -1))],
            7: [(3, (2,))],
        }[step]
        for phase, js in todo:
            for j in js:
                for half, d in hd2:
                    weight(kind, half, phase, j, d).wait_recv()

    def unit1(half, origin):
        d0 = pl.multiple_of(origin * 512 + half * 256, 256)
        r0 = pl.multiple_of(half * 256, 256)
        for n in range(3):
            cs = pl.ds(n * 256, 256)
            acc1[:, cs] += jnp.dot(
                tok[:, pl.ds(d0, 256)], w1[origin, pl.ds(r0, 256), cs],
                preferred_element_type=f32,
            )

        @pl.when(half == 1)
        def _():
            wp[pl.ds(0, 16), :] = w1[origin, pl.ds(512, 16), pl.ds(0, 512)]
            accd[...] += lax.dot_general(
                tok[pl.ds(0, 512), pl.ds(pl.multiple_of(origin * 512, 512), 512)],
                wp[...], NT, preferred_element_type=f32,
            )

    def unit2(half, origin):
        d0 = pl.multiple_of(origin * 512 + half * 256, 256)
        r0 = pl.multiple_of(half * 256, 256)
        for n in range(2):
            cs = pl.ds(n * 256, 256)
            acc2[:, cs] += jnp.dot(
                tok[pl.ds(0, 512), pl.ds(d0, 256)], w2[origin, pl.ds(r0, 256), cs],
                preferred_element_type=f32,
            )

    def multiply(kind, step):
        unit = (unit1, unit2)[kind]
        count = {0: 2, 1: 4, 2: 4, 3: 2, 4: 8, 5: 4, 6: 6, 7: 2}[step]

        def one(u, carry):
            half = lax.rem(u, 2)
            v = u // 2
            sign = 1 - 2 * lax.rem(v, 2)
            sign2 = 1 - 2 * (v // 2)
            rel = {
                0: (0, 0), 1: (sign, 0), 2: (0, sign), 3: (2, 0),
                4: (sign, sign2), 5: (2, sign), 6: (v - 1, 2), 7: (2, 2),
            }[step]
            unit(half, at(half, rel[0], rel[1]))
            return carry

        lax.fori_loop(0, count, one, 0)

    issue(0, 0)
    halo = remote(
        tok_hbm.at[pl.ds(512 - HALO, HALO), :], tok.at[pl.ds(512, HALO), :],
        hsend.at[0], hrecv.at[0], {"ctx": lax.rem(me + 1, 16)},
    )
    halo.start()
    for c in small_copies:
        c.wait()
    group = hd // 2

    def side(v):
        return jnp.where(core == 0, v[:, 0:256], v[:, 256:512])

    par[...] = jnp.zeros_like(par)
    par[0:5, 0:512] = convx[...]
    par[5:6, 0:512] = zxs[1:2, :]
    par[5:6, 512:768] = side(bcs[pl.ds(group, 1), :])
    for k in range(5):
        par[k:k + 1, 512:768] = side(convbc[k, pl.ds(group, 1), :])
    par[9:10, 0:512] = gain[...]
    par[10:11, 0:512] = zxs[0:1, :]
    left1 = lax.broadcasted_iota(jnp.int32, (1, 128), 1) < 64
    for p in range(4):
        par[11:12, p * 128:p * 128 + 128] = jnp.where(
            left1, hp[2:3, 2 * p:2 * p + 1], hp[2:3, 2 * p + 1:2 * p + 2]
        )
    par[12:13, 0:8] = hp[0:1, :]
    par[13:14, 0:8] = -jnp.exp(hp[1:2, :])
    par[21:24, 0:512] = tailx[...].astype(f32)
    mine = lax.broadcasted_iota(jnp.int32, (8, 512), 0) == group
    for k in range(3):
        chosen = jnp.where(mine, tailbc[k].astype(f32), 0.0)
        par[21 + k:22 + k, 512:768] = side(jnp.sum(chosen, axis=0, keepdims=True))
    acc1[...] = jnp.zeros_like(acc1)
    acc2[...] = jnp.zeros_like(acc2)
    accd[...] = jnp.zeros_like(accd)
    wp[...] = jnp.zeros_like(wp)
    tok_in.wait()
    w1_in.wait()
    w2_in.wait()
    halo.wait_recv()
    multiply(0, 0)
    for step in range(1, 6):
        arrive(0, step)
        issue(0, step)
        multiply(0, step)
    issue(1, 0)
    arrive(0, 6)
    multiply(0, 6)
    arrive(0, 7)
    multiply(0, 7)
    arrive(1, 1)
    issue(1, 1)

    scale = par[5:6, :]
    ext[8:520, :] = (acc1[0:512, :] * scale).astype(bf16).astype(f32)
    prev = (acc1[512:528, :] * scale).astype(bf16).astype(f32)
    first = jnp.where(me == 0, 1.0, 0.0).astype(f32)
    ext[0:8, :] = jnp.where(first > 0.5, par[16:24, :], prev[8:16, :])
    for r in range(4):
        summed = jnp.broadcast_to(par[4:5, :], (128, 768))
        for k in range(K):
            summed = summed + par[k:k + 1, :] * ext[5 + k + r * 128:5 + k + r * 128 + 128, :]
        act = (summed * (1.0 / (1.0 + jnp.exp(-summed)))).astype(bf16)
        xb[pl.ds(r * 128, 128), :] = act[:, 0:512]
        bcb[core, pl.ds(r * 128, 128), :] = act[:, 512:768]
    swap = remote(bcb.at[core], bcb.at[core], psend.at[0], precv.at[0], {"head": mate})
    swap.start()

    step_size = jax.nn.softplus(accd[...] + par[12:13, 0:128])
    rate_t = (step_size * par[13:14, 0:128]).T[0:16, :]
    lane = lax.broadcasted_iota(jnp.int32, (16, 512), 1)
    run = rate_t
    for s in (1, 2, 4, 8, 16, 32, 64, 128, 256):
        run = run + jnp.where(lane >= s, pltpu.roll(run, s, 1), 0.0)
    cumt[...] = run
    dtt[...] = step_size.T[0:16, :]
    cumc = jnp.concatenate([run, jnp.zeros((112, 512), f32)], 0).T
    cum[...] = cumc
    last = cumc[511:512, :]
    fade = jnp.exp(last - cumc) * step_size
    decay = jnp.exp(last)
    lanes = lax.broadcasted_iota(jnp.int32, (512, 128), 1)

    def by_head(cols, p):
        return jnp.where(lanes < 64, cols[:, 2 * p:2 * p + 1], cols[:, 2 * p + 1:2 * p + 2])

    swap.wait_recv()
    bpart = bcb[0]
    tag = lax.broadcasted_iota(jnp.int32, (16, 256), 0)
    for p in range(4):
        xf = (xb[:, pl.ds(p * 128, 128)].astype(f32) * by_head(fade, p)).astype(bf16)
        state = lax.dot_general(xf, bpart, TN, preferred_element_type=f32).astype(bf16)
        for q in range(4):
            piece = 4 * p + q
            h = piece // 2
            value = jnp.broadcast_to(decay[:, h:h + 1], (16, 256))
            hi = value.astype(bf16).astype(f32)
            mid = (value - hi).astype(bf16).astype(f32)
            low = value - hi - mid
            st1[piece, 0:32, :] = state[q * 32:q * 32 + 32, :]
            st1[piece, 32:48, :] = jnp.where(
                tag == 0, hi, jnp.where(tag == 1, mid, jnp.where(tag == 2, low, 0.0))
            ).astype(bf16)

    def exchange(src, dst, ssem, rsem):
        made_here = []
        for o in range(1, 16):
            who = lax.rem(me + o, 16)
            made_here.append(
                remote(src.at[who], dst.at[me], ssem.at[o - 1], rsem.at[o - 1], {"ctx": who})
            )
        return made_here

    ex1 = exchange(st1, rc1, as1, ar1)
    for c in ex1:
        c.start()
    rc1[me] = st1[me]
    arrive(1, 2)
    issue(1, 2)

    cpart = bcb[1]
    gs[...] = lax.dot_general(cpart, bpart, NT, preferred_element_type=f32)

    def pair(p):
        for i in range(2):
            size = 256 * (i + 1)
            rows = pl.ds(256 * i, 256)
            xp = xb[pl.ds(0, size), pl.ds(p * 128, 128)]
            lower = (
                lax.broadcasted_iota(jnp.int32, (256, size), 0) + 256 * i
                >= lax.broadcasted_iota(jnp.int32, (256, size), 1)
            )
            parts = []
            for h in (2 * p, 2 * p + 1):
                spread = cum[rows, h:h + 1] - cumt[h:h + 1, 0:size]
                e = jnp.exp(jnp.where(lower, spread, -1e30))
                m = (gs[rows, 0:size] * e * dtt[h:h + 1, 0:size]).astype(bf16)
                parts.append(jnp.dot(m, xp, preferred_element_type=f32))
            left = lax.broadcasted_iota(jnp.int32, (256, 128), 1) < 64
            cs = pl.ds(p * 128, 128)
            skip = par[11:12, p * 128:p * 128 + 128]
            yb[rows, cs] = jnp.where(left, parts[0], parts[1]) + skip * xb[rows, cs].astype(f32)

    pair(0)
    arrive(1, 3)
    issue(1, 3)
    for step in range(4):
        multiply(1, step)
    pair(1)

    for c in ex1:
        c.wait_recv()
    state = init[pl.ds(pl.multiple_of(me * 32, 32), 32), :]
    for i in range(16):
        st2[i] = state.astype(bf16)
        if i < 15:
            got = rc1[i].astype(f32)
            factor = got[32:33, :] + got[33:34, :] + got[34:35, :]
            state = factor * state + got[0:32, :]
    ex2 = exchange(st2, rc2, as2, ar2)
    for c in ex2:
        c.start()
    rc2[me] = st2[me]
    arrive(1, 4)
    issue(1, 4)
    pair(2)
    arrive(1, 5)
    issue(1, 5)
    pair(3)
    multiply(1, 4)
    multiply(1, 5)

    for c in ex2:
        c.wait_recv()
    grow = jnp.exp(cum[...])
    for p in range(4):
        cs = pl.ds(p * 128, 128)
        incoming = rc2[4 * p:4 * p + 4].reshape(128, 256)
        carried = lax.dot_general(cpart, incoming, NT, preferred_element_type=f32)
        yb[:, cs] += carried * by_head(grow, p)

    arrive(1, 6)
    multiply(1, 6)
    arrive(1, 7)
    multiply(1, 7)
    total = jnp.zeros((512, 128), f32)
    for p in range(4):
        cs = pl.ds(p * 128, 128)
        gate = (acc2[:, cs] * par[10:11, p * 128:p * 128 + 128]).astype(bf16).astype(f32)
        gated = yb[:, cs] * (gate * (1.0 / (1.0 + jnp.exp(-gate))))
        yb[:, cs] = gated
        total = total + gated * gated
    sq[core] = total
    swap2 = remote(sq.at[core], sq.at[core], psend.at[1], precv.at[1], {"head": mate})
    swap2.start()
    swap2.wait_recv()
    ms = jnp.sum(sq[0] + sq[1], axis=1, keepdims=True) * (1.0 / 1024.0)
    inv = lax.rsqrt(ms + 1e-05)
    for p in range(4):
        cs = pl.ds(p * 128, 128)
        out[:, cs] = (yb[:, cs] * inv * par[9:10, p * 128:p * 128 + 128]).astype(bf16)
    for c in sent:
        c.wait_send()


def body(
    tokens, w_zx, zx_scale, w_bc, bc_scale, w_dt, conv_x, conv_bc, tail_x, tail_bc,
    head_params, init_state, norm_gain,
):
    f32, bf16 = jnp.float32, jnp.bfloat16
    hd = lax.axis_index("head")
    group, core = hd // 2, hd % 2

    def pick(a):
        start = (0,) * (a.ndim - 2) + (group, core * 256)
        return lax.dynamic_slice(a, start, a.shape[:-2] + (1, 256)).reshape(a.shape[:-2] + (256,))

    w1 = jnp.concatenate(
        [
            jnp.concatenate([w_zx[:, 1, :], pick(w_bc)], 1),
            jnp.pad(w_dt.T, ((0, 8), (0, 256))),
        ],
        0,
    )
    w2 = w_zx[:, 0, :]

    vmem = pl.BlockSpec(memory_space=pltpu.VMEM)
    hbm = pl.BlockSpec(memory_space=pl.ANY)
    dma = pltpu.SemaphoreType.DMA
    small = (
        zx_scale, bc_scale, conv_x, conv_bc, tail_x, tail_bc, head_params,
        norm_gain.reshape(1, 512), init_state.reshape(512, 256),
    )
    return pl.pallas_call(
        kernel,
        out_shape=jax.ShapeDtypeStruct((512, 512), bf16),
        in_specs=[hbm] * 12,
        out_specs=vmem,
        scratch_shapes=[pltpu.VMEM(a.shape, a.dtype) for a in small] + [
            pltpu.VMEM((24, 768), f32),
            pltpu.VMEM((528, 8192), bf16),
            pltpu.VMEM((16, 528, 768), bf16),
            pltpu.VMEM((16, 512, 512), bf16),
            pltpu.VMEM((528, 768), f32),
            pltpu.VMEM((512, 512), f32),
            pltpu.VMEM((512, 128), f32),
            pltpu.VMEM((128, 512), bf16),
            pltpu.VMEM((520, 768), f32),
            pltpu.VMEM((512, 512), bf16),
            pltpu.VMEM((2, 512, 256), bf16),
            pltpu.VMEM((512, 512), f32),
            pltpu.VMEM((512, 512), f32),
            pltpu.VMEM((512, 128), f32),
            pltpu.VMEM((16, 512), f32),
            pltpu.VMEM((16, 512), f32),
            pltpu.VMEM((16, 48, 256), bf16),
            pltpu.VMEM((16, 48, 256), bf16),
            pltpu.VMEM((16, 32, 256), bf16),
            pltpu.VMEM((16, 32, 256), bf16),
            pltpu.VMEM((2, 512, 128), f32),
            dma((80,)), dma((80,)),
            dma((15,)), dma((15,)), dma((15,)), dma((15,)),
            dma((2,)), dma((2,)), dma((1,)), dma((1,)), dma((3,)), dma((9,)),
        ],
        compiler_params=pltpu.CompilerParams(
            collective_id=0, has_side_effects=True, vmem_limit_bytes=60 * 1024 * 1024
        ),
    )(tokens, w1, w2, *small)


def solution(mesh):
    return jax.shard_map(
        body,
        mesh=mesh,
        in_specs=(
            P("ctx", None),
            P("ctx", None, "head"),
            P(None, "head"),
            P("ctx", None, None),
            P(),
            P("ctx", "head"),
            P(None, "head"),
            P(),
            P(None, "head"),
            P(),
            P(None, "head"),
            P("head", None, None),
            P("head"),
        ),
        out_specs=P("ctx", "head"),
        check_vma=False,
    )
```
